32 devices in a mesh: grp: 2 (over y), pb: 4 (over z), re: 2 (over x), ka: 2 (over core).
Axes of the slice: x: 2, y: 2, z: 4, core: 2. Of those that a mesh axis runs over, the one named last changes fastest.
Arguments:
- g_wann: bfloat16 [2, 1024, 128, 256], P(None, 'pb', ('grp', 're'), 'ka'), parts along dimension 2, may hold values from -0.0234375 to 0.0234375
- phonon_phase: bfloat16 [2, 2048, 1024], P(None, 'pb'), may hold values from -1 to 1, as said below
- electron_phase: bfloat16 [2, 8, 64], replicated, may hold values from -1 to 1, as said below
Outputs:
- coupling: float32 [16, 2, 2048, 256], P(('grp', 're'), None, 'pb', 'ka'), parts along dimension 0
The draws below stay inside these ranges and needn't reach their ends.
There are 2 independent parts, one for each index of `grp`. The reference program is written for one: setup_inputs(seed, part) draws one part's arguments, and reference() takes and returns one part's arrays. A program takes and returns all parts, laid end to end along the dimension named above; an argument that names none is the same for every part. Nothing has to cross between parts.
Inputs may be any that keep to these rules, and one draw needn't show every extreme that they name: `phonon_phase`: entries 0 and 1 along the first dimension are the cosine and sine of one angle. `electron_phase`: entries 0 and 1 along the first dimension are the cosine and sine of one angle.
All inputs are finite; a program needn't handle non-finite values.
Results may differ from the reference program's by a relative error of at most 0.0029.
Values may be sent and summed in bfloat16 or wider, within the bound.
A program may use at most 64 MiB of HBM per device.

```python
import math
import jax
import jax.numpy as jnp
from jax import lax

BP = 256
RP = 1024
RE = 64
Q = 2048
K = 8


def phase_table(key, rows, vectors):
    key_moment, key_vector = jax.random.split(key)
    moment = jax.random.uniform(key_moment, (rows, 3), jnp.float32)
    picked = jax.random.permutation(key_vector, 4096)[:vectors]
    first = (picked // 256 - 8).astype(jnp.float32)
    second = (picked // 16 % 16 - 8).astype(jnp.float32)
    third = (picked % 16 - 8).astype(jnp.float32)
    product = moment[:, 0:1] * first[None, :] + moment[:, 1:2] * second[None, :] + moment[:, 2:3] * third[None, :]
    angle = 2.0 * math.pi * product
    return jnp.stack([jnp.cos(angle), jnp.sin(angle)]).astype(jnp.bfloat16)


def draw_phonon_phase(key, part):
    return phase_table(jax.random.fold_in(key, 101), Q, RP)


def draw_electron_phase(key, part):
    return phase_table(jax.random.fold_in(key, 202), K, RE)


def levels(key, extent, shards, low, largest):
    loudness = 1.0
    for axis_at, blocks in shards:
        steps = jax.random.uniform(jax.random.fold_in(jax.random.fold_in(key, 6), axis_at), (blocks,), jnp.float32, low / len(shards), largest / len(shards))
        loudness = loudness * jnp.repeat(jnp.exp(steps), extent[axis_at] // blocks).reshape((-1,) + (1,) * (len(extent) - 1 - axis_at))
    return loudness


def centred(stream_key, dims, width, bound, cuts=(), kind=jnp.bfloat16):
    drawn = jax.random.normal(stream_key, dims, jnp.float32) * width
    if len(cuts) > 0:
        drawn = levels(stream_key, dims, cuts, -0.22, 0.18) * drawn
    return jnp.clip(drawn, min=-bound, max=bound).astype(kind)


def setup_inputs(seed: int = 0, part: int = 0) -> dict:
    streams_of = jax.random.split(jax.random.key(seed), 4)
    part_keys = jax.random.split(jax.random.fold_in(streams_of[3], part), 4)
    return {
        "g_wann": centred(part_keys[0], (2, RP, RE, BP), (RE * RP) ** -0.5, 0.0234375, ((1, 4), (2, 2), (3, 2))),
        "phonon_phase": draw_phonon_phase(jax.random.fold_in(streams_of[3], 71), part),
        "electron_phase": draw_electron_phase(jax.random.fold_in(streams_of[3], 71), part),
    }


def reference(g_wann, phonon_phase, electron_phase):
    elec_cos = electron_phase[0].astype(jnp.float32)
    elec_sin = electron_phase[1].astype(jnp.float32)
    wann_real = g_wann[0].astype(jnp.float32)
    wann_imag = g_wann[1].astype(jnp.float32)
    high = lax.Precision.HIGHEST
    bloch_real = jnp.einsum("ke,peb->kpb", elec_cos, wann_real, precision=high) - jnp.einsum("ke,peb->kpb", elec_sin, wann_imag, precision=high)
    bloch_imag = jnp.einsum("ke,peb->kpb", elec_cos, wann_imag, precision=high) + jnp.einsum("ke,peb->kpb", elec_sin, wann_real, precision=high)
    bloch_real = bloch_real.astype(jnp.bfloat16)
    bloch_imag = bloch_imag.astype(jnp.bfloat16)
    cos_table = phonon_phase[0]
    sin_table = phonon_phase[1]

    def one_moment(pair):
        part_real, part_imag = pair
        out_real = jnp.dot(cos_table, part_real, preferred_element_type=jnp.float32) - jnp.dot(sin_table, part_imag, preferred_element_type=jnp.float32)
        out_imag = jnp.dot(cos_table, part_imag, preferred_element_type=jnp.float32) + jnp.dot(sin_table, part_real, preferred_element_type=jnp.float32)
        return jnp.stack([out_real, out_imag])

    return lax.map(one_moment, (bloch_real, bloch_imag))
```

```python
import functools
import jax
import jax.numpy as jnp
from jax import lax
from jax.experimental import pallas as pl
from jax.experimental.pallas import tpu as pltpu
from jax.sharding import PartitionSpec as P

MESH = pl.DeviceIdType.MESH
GROUP = 8
BF16 = jnp.bfloat16
F32 = jnp.float32


def iota(shape, dim):
    return lax.broadcasted_iota(jnp.int32, shape, dim)


def kernel(
    n_re, n_pb, halves,
    g_hbm, ph_hbm, el_ref, out_hbm,
    g, ph, el_block, part, x_recv, gath, out,
    g_sem, ph_sem, out_sem, x_send, x_got, z_send, z_got,
):
    x = lax.axis_index("re")
    z = lax.axis_index("pb")
    k_all, p_loc, width = part.shape
    b = width // 2
    k_own = k_all // n_re
    p_half = p_loc // halves
    e_all = el_ref.shape[2]
    e_loc = g.shape[1] // p_loc
    chunks = k_own * halves
    q_loc = ph.shape[1]

    def g_copy(h):
        rows = pl.ds(h * p_half * e_loc, p_half * e_loc)
        return pltpu.make_async_copy(g_hbm.at[:, rows, :], g.at[:, rows, :], g_sem.at[h])

    for h in range(halves):
        g_copy(h).start()
    ph_copy = pltpu.make_async_copy(ph_hbm, ph, ph_sem)
    ph_copy.start()

    barrier = pltpu.get_barrier_semaphore()
    for d in range(1, n_re):
        pl.semaphore_signal(barrier, inc=1, device_id={"re": lax.rem(x + d, n_re)}, device_id_type=MESH)

    @pl.when(z > 0)
    def _():
        pl.semaphore_signal(barrier, inc=1, device_id={"pb": z - 1}, device_id_type=MESH)

    @pl.when(z < n_pb - 1)
    def _():
        pl.semaphore_signal(barrier, inc=1, device_id={"pb": z + 1}, device_id_type=MESH)

    rows, cols = k_all * GROUP, GROUP * e_loc
    spread_k = (iota((rows, k_all), 0) // GROUP == iota((rows, k_all), 1)).astype(BF16)
    spread_e = (iota((e_all, cols), 0) == x * e_loc + iota((e_all, cols), 1) % e_loc).astype(BF16)
    same_p = iota((rows, cols), 0) % GROUP == iota((rows, cols), 1) // e_loc

    def spread(table):
        t = jnp.dot(spread_k, table, preferred_element_type=F32).astype(BF16)
        t = jnp.dot(t, spread_e, preferred_element_type=F32)
        return jnp.where(same_p, t, 0.0)

    cos_e = spread(el_ref[0])
    sin_e = spread(el_ref[1])
    el_block[0:rows, 0:cols] = cos_e.astype(BF16)
    el_block[0:rows, cols:] = (-sin_e).astype(BF16)
    el_block[rows:, 0:cols] = sin_e.astype(BF16)
    el_block[rows:, cols:] = cos_e.astype(BF16)

    n_meet = n_re - 1 + jnp.where(z > 0, 1, 0) + jnp.where(z < n_pb - 1, 1, 0)
    pl.semaphore_wait(barrier, n_meet)

    def x_copy(c, d):
        k, h = c // halves, c % halves
        there = pl.ds(pl.multiple_of(h * p_half, p_half), p_half)
        to = lax.rem(x + d, n_re)
        return pltpu.make_async_remote_copy(
            src_ref=part.at[to * k_own + k, there, :],
            dst_ref=x_recv.at[d - 1, k, there, :],
            send_sem=x_send.at[d - 1, c],
            recv_sem=x_got.at[d - 1, c],
            device_id={"re": to},
            device_id_type=MESH,
        )

    for h in range(halves):
        g_copy(h).wait()

        @pl.loop(h * (p_half // GROUP), (h + 1) * (p_half // GROUP), unroll=2)
        def _(j):
            at = pl.ds(pl.multiple_of(j * cols, cols), cols)
            both = jnp.concatenate([g[0, at, :], g[1, at, :]], axis=0)
            res = jnp.dot(el_block[...], both, preferred_element_type=F32)
            p_at = pl.ds(pl.multiple_of(j * GROUP, GROUP), GROUP)
            for c in range(2):
                for k in range(k_all):
                    first = (c * k_all + k) * GROUP
                    part[k, p_at, c * b:(c + 1) * b] = res[first:first + GROUP]

        for d in range(1, n_re):
            x_copy(h, d).start()
    for c in range(halves, chunks):
        for d in range(1, n_re):
            x_copy(c, d).start()

    def z_copy(c, source, way):
        k, h = c // halves, c % halves
        there = pl.ds(pl.multiple_of(source * p_loc + h * p_half, p_half), p_half)
        block = gath.at[k, there, :]
        return pltpu.make_async_remote_copy(
            src_ref=block,
            dst_ref=block,
            send_sem=z_send.at[way, c, source],
            recv_sem=z_got.at[c, source],
            device_id={"pb": z + 1 if way else z - 1},
            device_id_type=MESH,
        )

    @pl.loop(0, chunks + n_pb - 2)
    def _(t):
        @pl.when(t < chunks)
        def _():
            k, h = t // halves, t % halves
            there = pl.ds(pl.multiple_of(h * p_half, p_half), p_half)
            for d in range(1, n_re):
                x_copy(t, d).wait_recv()
            total = part[x * k_own + k, there, :]
            for d in range(1, n_re):
                total = total + x_recv[d - 1, k, there, :]
            mine = pl.ds(pl.multiple_of(z * p_loc + h * p_half, p_half), p_half)
            gath[k, mine, :] = total.astype(BF16)

            @pl.when(z > 0)
            def _():
                z_copy(t, z, 0).start()

            @pl.when(z < n_pb - 1)
            def _():
                z_copy(t, z, 1).start()

        for d in range(1, n_pb - 1):
            c = t - d
            ok = (c >= 0) & (c < chunks)

            @pl.when(ok & (z - d >= 0) & (z < n_pb - 1))
            def _():
                z_copy(c, z - d, 1).wait_recv()
                z_copy(c, z - d, 1).start()

            @pl.when(ok & (z + d < n_pb) & (z > 0))
            def _():
                z_copy(c, z + d, 0).wait_recv()
                z_copy(c, z + d, 0).start()

    ph_copy.wait()
    q_tile = min(256, q_loc)

    def out_copy(k):
        return pltpu.make_async_copy(out.at[k], out_hbm.at[k], out_sem.at[k])

    @pl.loop(0, k_own)
    def _(k):
        for h in range(halves):
            c = k * halves + h
            for s in range(n_pb):
                @pl.when(((s < z) & (z == n_pb - 1)) | ((s > z) & (z == 0)))
                def _():
                    z_copy(c, s, 0).wait_recv()

        @pl.loop(0, q_loc // q_tile)
        def _(i):
            at = pl.ds(pl.multiple_of(i * q_tile, q_tile), q_tile)
            data = gath[k]
            by_cos = jnp.dot(ph[0, at, :], data, preferred_element_type=F32)
            by_sin = jnp.dot(ph[1, at, :], data, preferred_element_type=F32)
            out[k, 0, at, :] = by_cos[:, :b] - by_sin[:, b:]
            out[k, 1, at, :] = by_cos[:, b:] + by_sin[:, :b]

        out_copy(k).start()

    @pl.loop(0, chunks)
    def _(c):
        for d in range(1, n_re):
            x_copy(c, d).wait_send()
        for s in range(n_pb):
            @pl.when((s >= z) & (z > 0))
            def _():
                z_copy(c, s, 0).wait_send()

            @pl.when((s <= z) & (z < n_pb - 1))
            def _():
                z_copy(c, s, 1).wait_send()

    for k in range(k_own):
        out_copy(k).wait()


def body(n_re, n_pb, g_wann, phonon_phase, electron_phase):
    _, p_loc, e_loc, b = g_wann.shape
    _, q_loc, p_all = phonon_phase.shape
    k_all = electron_phase.shape[1]
    k_own = k_all // n_re
    halves = 2
    chunks = k_own * halves
    g = g_wann.reshape(2, p_loc * e_loc, b)
    anywhere = pl.BlockSpec(memory_space=pl.ANY)
    return pl.pallas_call(
        functools.partial(kernel, n_re, n_pb, halves),
        out_shape=jax.ShapeDtypeStruct((k_own, 2, q_loc, b), F32),
        in_specs=[anywhere, anywhere, pl.BlockSpec(memory_space=pltpu.VMEM)],
        out_specs=anywhere,
        scratch_shapes=[
            pltpu.VMEM(g.shape, BF16),
            pltpu.VMEM(phonon_phase.shape, BF16),
            pltpu.VMEM((2 * k_all * GROUP, 2 * GROUP * e_loc), BF16),
            pltpu.VMEM((k_all, p_loc, 2 * b), F32),
            pltpu.VMEM((n_re - 1, k_own, p_loc, 2 * b), F32),
            pltpu.VMEM((k_own, p_all, 2 * b), BF16),
            pltpu.VMEM((k_own, 2, q_loc, b), F32),
            pltpu.SemaphoreType.DMA((halves,)),
            pltpu.SemaphoreType.DMA,
            pltpu.SemaphoreType.DMA((k_own,)),
            pltpu.SemaphoreType.DMA((n_re - 1, chunks)),
            pltpu.SemaphoreType.DMA((n_re - 1, chunks)),
            pltpu.SemaphoreType.DMA((2, chunks, n_pb)),
            pltpu.SemaphoreType.DMA((chunks, n_pb)),
        ],
        compiler_params=pltpu.CompilerParams(
            collective_id=0, has_side_effects=True, vmem_limit_bytes=60 * 1024 * 1024
        ),
    )(g, phonon_phase, electron_phase)


def solution(mesh):
    placed = (P(None, "pb", ("grp", "re"), "ka"), P(None, "pb", None), P())
    return jax.shard_map(
        functools.partial(body, mesh.shape["re"], mesh.shape["pb"]),
        mesh=mesh,
        in_specs=placed,
        out_specs=P(("grp", "re"), None, "pb", "ka"),
        check_vma=False,
    )
```

```python
import functools
import jax
import jax.numpy as jnp
from jax import lax
from jax.experimental import pallas as pl
from jax.experimental.pallas import tpu as pltpu
from jax.sharding import PartitionSpec as P

MESH = pl.DeviceIdType.MESH
GROUP = 8
BF16 = jnp.bfloat16
F32 = jnp.float32


def iota(shape, dim):
    return lax.broadcasted_iota(jnp.int32, shape, dim)


def kernel(
    n_re, n_pb, halves,
    g_hbm, ph_hbm, el_ref, out,
    g, ph, el_block, part, x_first, x_first_recv, x_recv, gath,
    g_sem, ph_sem, x_send, x_got, z_send, z_got,
):
    x = lax.axis_index("re")
    z = lax.axis_index("pb")
    k_all, p_loc, width = part.shape
    b = width // 2
    k_own = k_all // n_re
    p_half = p_loc // halves
    e_all = el_ref.shape[2]
    e_loc = g.shape[1] // p_loc
    chunks = k_own * halves
    q_loc = ph.shape[1]

    def g_copy(h):
        rows = pl.ds(h * p_half * e_loc, p_half * e_loc)
        return pltpu.make_async_copy(g_hbm.at[:, rows, :], g.at[:, rows, :], g_sem.at[h])

    for h in range(halves):
        g_copy(h).start()
    ph_copy = pltpu.make_async_copy(ph_hbm, ph, ph_sem)
    ph_copy.start()

    barrier = pltpu.get_barrier_semaphore()
    for d in range(1, n_re):
        pl.semaphore_signal(barrier, inc=1, device_id={"re": lax.rem(x + d, n_re)}, device_id_type=MESH)

    @pl.when(z > 0)
    def _():
        pl.semaphore_signal(barrier, inc=1, device_id={"pb": z - 1}, device_id_type=MESH)

    @pl.when(z < n_pb - 1)
    def _():
        pl.semaphore_signal(barrier, inc=1, device_id={"pb": z + 1}, device_id_type=MESH)

    rows, cols = k_all * GROUP, GROUP * e_loc
    spread_k = (iota((rows, k_all), 0) // GROUP == iota((rows, k_all), 1)).astype(BF16)
    spread_e = (iota((e_all, cols), 0) == x * e_loc + iota((e_all, cols), 1) % e_loc).astype(BF16)
    same_p = iota((rows, cols), 0) % GROUP == iota((rows, cols), 1) // e_loc

    def spread(table):
        t = jnp.dot(spread_k, table, preferred_element_type=F32).astype(BF16)
        t = jnp.dot(t, spread_e, preferred_element_type=F32)
        return jnp.where(same_p, t, 0.0)

    cos_e = spread(el_ref[0])
    sin_e = spread(el_ref[1])
    el_block[0:rows, 0:cols] = cos_e.astype(BF16)
    el_block[0:rows, cols:] = (-sin_e).astype(BF16)
    el_block[rows:, 0:cols] = sin_e.astype(BF16)
    el_block[rows:, cols:] = cos_e.astype(BF16)

    n_meet = n_re - 1 + jnp.where(z > 0, 1, 0) + jnp.where(z < n_pb - 1, 1, 0)
    pl.semaphore_wait(barrier, n_meet)

    def x_first_copy(h, d):
        there = pl.ds(pl.multiple_of(h * p_half, p_half), p_half)
        to = lax.rem(x + d, n_re)
        return pltpu.make_async_remote_copy(
            src_ref=x_first.at[to, there, :],
            dst_ref=x_first_recv.at[d - 1, there, :],
            send_sem=x_send.at[d - 1, h],
            recv_sem=x_got.at[d - 1, h],
            device_id={"re": to},
            device_id_type=MESH,
        )

    def x_copy(c, d):
        k, h = c // halves, c % halves
        there = pl.ds(pl.multiple_of(h * p_half, p_half), p_half)
        to = lax.rem(x + d, n_re)
        return pltpu.make_async_remote_copy(
            src_ref=part.at[to * k_own + k, there, :],
            dst_ref=x_recv.at[d - 1, k, there, :],
            send_sem=x_send.at[d - 1, c],
            recv_sem=x_got.at[d - 1, c],
            device_id={"re": to},
            device_id_type=MESH,
        )

    for h in range(halves):
        g_copy(h).wait()

        @pl.loop(h * (p_half // GROUP), (h + 1) * (p_half // GROUP), unroll=2)
        def _(j):
            at = pl.ds(pl.multiple_of(j * cols, cols), cols)
            both = jnp.concatenate([g[0, at, :], g[1, at, :]], axis=0)
            res = jnp.dot(el_block[...], both, preferred_element_type=F32)
            p_at = pl.ds(pl.multiple_of(j * GROUP, GROUP), GROUP)
            for c in range(2):
                for k in range(k_all):
                    first = (c * k_all + k) * GROUP
                    part[k, p_at, c * b:(c + 1) * b] = res[first:first + GROUP]

        there = pl.ds(h * p_half, p_half)
        for r in range(n_re):
            x_first[r, there, :] = part[r * k_own, there, :].astype(BF16)
        for d in range(1, n_re):
            x_first_copy(h, d).start()
    for c in range(halves, chunks):
        for d in range(1, n_re):
            x_copy(c, d).start()

    def z_copy(c, source, way):
        k, h = c // halves, c % halves
        there = pl.ds(pl.multiple_of(source * p_loc + h * p_half, p_half), p_half)
        block = gath.at[k, there, :]
        return pltpu.make_async_remote_copy(
            src_ref=block,
            dst_ref=block,
            send_sem=z_send.at[way, c, source],
            recv_sem=z_got.at[c, source],
            device_id={"pb": z + 1 if way else z - 1},
            device_id_type=MESH,
        )

    @pl.loop(0, chunks + n_pb - 2)
    def _(t):
        @pl.when(t < chunks)
        def _():
            k, h = t // halves, t % halves
            there = pl.ds(pl.multiple_of(h * p_half, p_half), p_half)
            mine = pl.ds(pl.multiple_of(z * p_loc + h * p_half, p_half), p_half)

            @pl.when(t < halves)
            def _():
                total = part[x * k_own, there, :]
                for d in range(1, n_re):
                    x_first_copy(t, d).wait_recv()
                    total = total + x_first_recv[d - 1, there, :].astype(F32)
                gath[0, mine, :] = total.astype(BF16)

            @pl.when(t >= halves)
            def _():
                total = part[x * k_own + k, there, :]
                for d in range(1, n_re):
                    x_copy(t, d).wait_recv()
                    total = total + x_recv[d - 1, k, there, :]
                gath[k, mine, :] = total.astype(BF16)

            @pl.when(z > 0)
            def _():
                z_copy(t, z, 0).start()

            @pl.when(z < n_pb - 1)
            def _():
                z_copy(t, z, 1).start()

        for d in range(1, n_pb - 1):
            c = t - d
            ok = (c >= 0) & (c < chunks)

            @pl.when(ok & (z - d >= 0) & (z < n_pb - 1))
            def _():
                z_copy(c, z - d, 1).wait_recv()
                z_copy(c, z - d, 1).start()

            @pl.when(ok & (z + d < n_pb) & (z > 0))
            def _():
                z_copy(c, z + d, 0).wait_recv()
                z_copy(c, z + d, 0).start()

    ph_copy.wait()
    q_tile = min(256, q_loc)

    @pl.loop(0, k_own)
    def _(k):
        for h in range(halves):
            c = k * halves + h
            for s in range(n_pb):
                @pl.when(((s < z) & (z == n_pb - 1)) | ((s > z) & (z == 0)))
                def _():
                    z_copy(c, s, 0).wait_recv()

        @pl.loop(0, q_loc // q_tile)
        def _(i):
            at = pl.ds(pl.multiple_of(i * q_tile, q_tile), q_tile)
            data = gath[k]
            by_cos = jnp.dot(ph[0, at, :], data, preferred_element_type=F32)
            by_sin = jnp.dot(ph[1, at, :], data, preferred_element_type=F32)
            out[k, 0, at, :] = by_cos[:, :b] - by_sin[:, b:]
            out[k, 1, at, :] = by_cos[:, b:] + by_sin[:, :b]

    @pl.loop(0, chunks)
    def _(c):
        for d in range(1, n_re):
            @pl.when(c < halves)
            def _():
                x_first_copy(c, d).wait_send()

            @pl.when(c >= halves)
            def _():
                x_copy(c, d).wait_send()
        for s in range(n_pb):
            @pl.when((s >= z) & (z > 0))
            def _():
                z_copy(c, s, 0).wait_send()

            @pl.when((s <= z) & (z < n_pb - 1))
            def _():
                z_copy(c, s, 1).wait_send()


def body(n_re, n_pb, g_wann, phonon_phase, electron_phase):
    _, p_loc, e_loc, b = g_wann.shape
    _, q_loc, p_all = phonon_phase.shape
    k_all = electron_phase.shape[1]
    k_own = k_all // n_re
    halves = 4
    chunks = k_own * halves
    g = g_wann.reshape(2, p_loc * e_loc, b)
    far = pl.BlockSpec(memory_space=pltpu.HBM)
    near = pl.BlockSpec(memory_space=pltpu.VMEM)
    return pl.pallas_call(
        functools.partial(kernel, n_re, n_pb, halves),
        out_shape=jax.ShapeDtypeStruct((k_own, 2, q_loc, b), F32),
        in_specs=[far, far, near],
        out_specs=near,
        scratch_shapes=[
            pltpu.VMEM(g.shape, BF16),
            pltpu.VMEM(phonon_phase.shape, BF16),
            pltpu.VMEM((2 * k_all * GROUP, 2 * GROUP * e_loc), BF16),
            pltpu.VMEM((k_all, p_loc, 2 * b), F32),
            pltpu.VMEM((n_re, p_loc, 2 * b), BF16),
            pltpu.VMEM((n_re - 1, p_loc, 2 * b), BF16),
            pltpu.VMEM((n_re - 1, k_own, p_loc, 2 * b), F32),
            pltpu.VMEM((k_own, p_all, 2 * b), BF16),
            pltpu.SemaphoreType.DMA((halves,)),
            pltpu.SemaphoreType.DMA,
            pltpu.SemaphoreType.DMA((n_re - 1, chunks)),
            pltpu.SemaphoreType.DMA((n_re - 1, chunks)),
            pltpu.SemaphoreType.DMA((2, chunks, n_pb)),
            pltpu.SemaphoreType.DMA((chunks, n_pb)),
        ],
        compiler_params=pltpu.CompilerParams(
            collective_id=0, has_side_effects=True, vmem_limit_bytes=24 * 1024 * 1024
        ),
    )(*(pltpu.with_memory_space_constraint(a, pltpu.HBM) for a in (g, phonon_phase, electron_phase)))


def solution(mesh):
    placed = (P(None, "pb", ("grp", "re"), "ka"), P(None, "pb", None), P())
    return jax.shard_map(
        functools.partial(body, mesh.shape["re"], mesh.shape["pb"]),
        mesh=mesh,
        in_specs=placed,
        out_specs=P(("grp", "re"), None, "pb", "ka"),
        check_vma=False,
    )
```

```python
import functools
import jax
import jax.numpy as jnp
from jax import lax
from jax.experimental import pallas as pl
from jax.experimental.pallas import tpu as pltpu
from jax.sharding import PartitionSpec as P

MESH = pl.DeviceIdType.MESH
GROUP = 8
PAIR = 2
SLACK = 2
BF16 = jnp.bfloat16
F32 = jnp.float32


def iota(shape, dim):
    return lax.broadcasted_iota(jnp.int32, shape, dim)


def kernel(
    n_re, n_pb, halves,
    g_hbm, ph_hbm, el_ref, out,
    g, ph, el_block, part, x_first, x_first_recv, x_recv, gath,
    g_sem, ph_sem, x_send, x_got, z_send, z_got,
):
    x = lax.axis_index("re")
    z = lax.axis_index("pb")
    k_all, p_loc, width = part.shape
    b = width // 2
    k_own = k_all // n_re
    p_half = p_loc // halves
    e_all = el_ref.shape[2]
    e_loc = g.shape[1] // p_loc
    chunks = k_own * halves
    q_loc = ph.shape[1]

    def g_copy(h):
        rows = pl.ds(h * p_half * e_loc, p_half * e_loc)
        return pltpu.make_async_copy(g_hbm.at[:, rows, :], g.at[:, rows, :], g_sem.at[h])

    for h in range(halves):
        g_copy(h).start()

    barrier = pltpu.get_barrier_semaphore()
    for d in range(1, n_re):
        pl.semaphore_signal(barrier, inc=1, device_id={"re": lax.rem(x + d, n_re)}, device_id_type=MESH)

    @pl.when(z > 0)
    def _():
        pl.semaphore_signal(barrier, inc=1, device_id={"pb": z - 1}, device_id_type=MESH)

    @pl.when(z < n_pb - 1)
    def _():
        pl.semaphore_signal(barrier, inc=1, device_id={"pb": z + 1}, device_id_type=MESH)

    rows, cols = k_all * GROUP, GROUP * e_loc
    spread_k = (iota((rows, k_all), 0) // GROUP == iota((rows, k_all), 1)).astype(BF16)
    spread_e = (iota((e_all, cols), 0) == x * e_loc + iota((e_all, cols), 1) % e_loc).astype(BF16)
    same_p = iota((rows, cols), 0) % GROUP == iota((rows, cols), 1) // e_loc

    def spread(table):
        t = jnp.dot(spread_k, table, preferred_element_type=F32).astype(BF16)
        t = jnp.dot(t, spread_e, preferred_element_type=F32)
        return jnp.where(same_p, t, 0.0)

    cos_e = spread(el_ref[0])
    sin_e = spread(el_ref[1])
    el_block[0:rows, 0:cols] = cos_e.astype(BF16)
    el_block[0:rows, cols:] = (-sin_e).astype(BF16)
    el_block[rows:, 0:cols] = sin_e.astype(BF16)
    el_block[rows:, cols:] = cos_e.astype(BF16)

    def x_first_copy(h, d):
        there = pl.ds(pl.multiple_of(h * p_half, p_half), p_half)
        to = lax.rem(x + d, n_re)
        return pltpu.make_async_remote_copy(
            src_ref=x_first.at[to, there, :],
            dst_ref=x_first_recv.at[d - 1, there, :],
            send_sem=x_send.at[d - 1, h],
            recv_sem=x_got.at[d - 1, h],
            device_id={"re": to},
            device_id_type=MESH,
        )

    def x_copy(c, d):
        k, h = c // halves, c % halves
        there = pl.ds(pl.multiple_of(h * p_half, p_half), p_half)
        to = lax.rem(x + d, n_re)
        return pltpu.make_async_remote_copy(
            src_ref=part.at[to * k_own + k, there, :],
            dst_ref=x_recv.at[d - 1, k, there, :],
            send_sem=x_send.at[d - 1, c],
            recv_sem=x_got.at[d - 1, c],
            device_id={"re": to},
            device_id_type=MESH,
        )

    for h in range(halves):
        g_copy(h).wait()

        @pl.loop(h * (p_half // GROUP // PAIR), (h + 1) * (p_half // GROUP // PAIR), unroll=2)
        def _(j):
            sides = []
            for side in range(PAIR):
                at = pl.ds(pl.multiple_of((j * PAIR + side) * cols, cols), cols)
                sides.append(jnp.concatenate([g[0, at, :], g[1, at, :]], axis=0))
            both = jnp.concatenate(sides, axis=1)
            res = jnp.dot(el_block[...], both, preferred_element_type=F32)
            for side in range(PAIR):
                p_at = pl.ds(pl.multiple_of((j * PAIR + side) * GROUP, GROUP), GROUP)
                for c in range(2):
                    for k in range(k_all):
                        first = (c * k_all + k) * GROUP
                        part[k, p_at, c * b:(c + 1) * b] = res[first:first + GROUP, side * b:(side + 1) * b]

        if h == 0:
            n_meet = n_re - 1 + jnp.where(z > 0, 1, 0) + jnp.where(z < n_pb - 1, 1, 0)
            pl.semaphore_wait(barrier, n_meet)
        there = pl.ds(h * p_half, p_half)
        for r in range(n_re):
            x_first[r, there, :] = part[r * k_own, there, :].astype(BF16)
        for d in range(1, n_re):
            x_first_copy(h, d).start()
    for c in range(halves, chunks):
        for d in range(1, n_re):
            x_copy(c, d).start()
    ph_copy = pltpu.make_async_copy(ph_hbm, ph, ph_sem)
    ph_copy.start()

    def z_copy(c, source, way):
        k, h = c // halves, c % halves
        there = pl.ds(pl.multiple_of(source * p_loc + h * p_half, p_half), p_half)
        block = gath.at[k, there, :]
        return pltpu.make_async_remote_copy(
            src_ref=block,
            dst_ref=block,
            send_sem=z_send.at[way, c, source],
            recv_sem=z_got.at[c, source],
            device_id={"pb": z + 1 if way else z - 1},
            device_id_type=MESH,
        )

    @pl.loop(0, chunks + (n_pb - 2) * (1 + SLACK))
    def _(t):
        @pl.when(t < chunks)
        def _():
            k, h = t // halves, t % halves
            there = pl.ds(pl.multiple_of(h * p_half, p_half), p_half)
            mine = pl.ds(pl.multiple_of(z * p_loc + h * p_half, p_half), p_half)

            @pl.when(t < halves)
            def _():
                total = part[x * k_own, there, :]
                for d in range(1, n_re):
                    x_first_copy(t, d).wait_recv()
                    total = total + x_first_recv[d - 1, there, :].astype(F32)
                gath[0, mine, :] = total.astype(BF16)

            @pl.when(t >= halves)
            def _():
                total = part[x * k_own + k, there, :]
                for d in range(1, n_re):
                    x_copy(t, d).wait_recv()
                    total = total + x_recv[d - 1, k, there, :]
                gath[k, mine, :] = total.astype(BF16)

            @pl.when(z > 0)
            def _():
                z_copy(t, z, 0).start()

            @pl.when(z < n_pb - 1)
            def _():
                z_copy(t, z, 1).start()

        for d in range(1, n_pb - 1):
            c = t - d * (1 + SLACK)
            ok = (c >= 0) & (c < chunks)

            @pl.when(ok & (z - d >= 0) & (z < n_pb - 1))
            def _():
                z_copy(c, z - d, 1).wait_recv()
                z_copy(c, z - d, 1).start()

            @pl.when(ok & (z + d < n_pb) & (z > 0))
            def _():
                z_copy(c, z + d, 0).wait_recv()
                z_copy(c, z + d, 0).start()

    ph_copy.wait()
    q_tile = min(256, q_loc)

    @pl.loop(0, k_own)
    def _(k):
        for h in range(halves):
            c = k * halves + h
            for s in range(n_pb):
                @pl.when(((s < z) & (z == n_pb - 1)) | ((s > z) & (z == 0)))
                def _():
                    z_copy(c, s, 0).wait_recv()

        @pl.loop(0, q_loc // q_tile)
        def _(i):
            at = pl.ds(pl.multiple_of(i * q_tile, q_tile), q_tile)
            data = gath[k]
            by_cos = jnp.dot(ph[0, at, :], data, preferred_element_type=F32)
            by_sin = jnp.dot(ph[1, at, :], data, preferred_element_type=F32)
            out[k, 0, at, :] = by_cos[:, :b] - by_sin[:, b:]
            out[k, 1, at, :] = by_cos[:, b:] + by_sin[:, :b]

    @pl.loop(0, chunks)
    def _(c):
        for d in range(1, n_re):
            @pl.when(c < halves)
            def _():
                x_first_copy(c, d).wait_send()

            @pl.when(c >= halves)
            def _():
                x_copy(c, d).wait_send()
        for s in range(n_pb):
            @pl.when((s >= z) & (z > 0))
            def _():
                z_copy(c, s, 0).wait_send()

            @pl.when((s <= z) & (z < n_pb - 1))
            def _():
                z_copy(c, s, 1).wait_send()


def body(n_re, n_pb, g_wann, phonon_phase, electron_phase):
    _, p_loc, e_loc, b = g_wann.shape
    _, q_loc, p_all = phonon_phase.shape
    k_all = electron_phase.shape[1]
    k_own = k_all // n_re
    halves = 4
    chunks = k_own * halves
    g = g_wann.reshape(2, p_loc * e_loc, b)
    far = pl.BlockSpec(memory_space=pltpu.HBM)
    near = pl.BlockSpec(memory_space=pltpu.VMEM)
    return pl.pallas_call(
        functools.partial(kernel, n_re, n_pb, halves),
        out_shape=jax.ShapeDtypeStruct((k_own, 2, q_loc, b), F32),
        in_specs=[far, far, near],
        out_specs=near,
        scratch_shapes=[
            pltpu.VMEM(g.shape, BF16),
            pltpu.VMEM(phonon_phase.shape, BF16),
            pltpu.VMEM((2 * k_all * GROUP, 2 * GROUP * e_loc), BF16),
            pltpu.VMEM((k_all, p_loc, 2 * b), F32),
            pltpu.VMEM((n_re, p_loc, 2 * b), BF16),
            pltpu.VMEM((n_re - 1, p_loc, 2 * b), BF16),
            pltpu.VMEM((n_re - 1, k_own, p_loc, 2 * b), F32),
            pltpu.VMEM((k_own, p_all, 2 * b), BF16),
            pltpu.SemaphoreType.DMA((halves,)),
            pltpu.SemaphoreType.DMA,
            pltpu.SemaphoreType.DMA((n_re - 1, chunks)),
            pltpu.SemaphoreType.DMA((n_re - 1, chunks)),
            pltpu.SemaphoreType.DMA((2, chunks, n_pb)),
            pltpu.SemaphoreType.DMA((chunks, n_pb)),
        ],
        compiler_params=pltpu.CompilerParams(
            collective_id=0, has_side_effects=True, vmem_limit_bytes=24 * 1024 * 1024
        ),
    )(*(pltpu.with_memory_space_constraint(a, pltpu.HBM) for a in (g, phonon_phase, electron_phase)))


def solution(mesh):
    placed = (P(None, "pb", ("grp", "re"), "ka"), P(None, "pb", None), P())
    return jax.shard_map(
        functools.partial(body, mesh.shape["re"], mesh.shape["pb"]),
        mesh=mesh,
        in_specs=placed,
        out_specs=P(("grp", "re"), None, "pb", "ka"),
        check_vma=False,
    )
```

```python
import functools
import jax
import jax.numpy as jnp
from jax import lax
from jax.experimental import pallas as pl
from jax.experimental.pallas import tpu as pltpu
from jax.sharding import PartitionSpec as P

MESH = pl.DeviceIdType.MESH
GROUP = 8
PAIR = 2
UNROLL = 4
AHEAD = 1
SLACK = 0
BF16 = jnp.bfloat16
F32 = jnp.float32


def iota(shape, dim):
    return lax.broadcasted_iota(jnp.int32, shape, dim)


def kernel(
    n_re, n_pb, halves,
    g_hbm, ph_hbm, el_hbm, out,
    g, ph, el_ref, el_block, part, x_first, x_first_recv, x_recv, gath,
    g_sem, ph_sem, el_sem, x_send, x_got, z_send, z_got,
):
    x = lax.axis_index("re")
    z = lax.axis_index("pb")
    k_all, p_loc, width = part.shape
    b = width // 2
    k_own = k_all // n_re
    p_half = p_loc // halves
    e_all = el_ref.shape[2]
    e_loc = g.shape[1] // p_loc
    chunks = k_own * halves
    q_loc = ph.shape[1]

    def g_copy(h):
        rows = pl.ds(h * p_half * e_loc, p_half * e_loc)
        return pltpu.make_async_copy(g_hbm.at[:, rows, :], g.at[:, rows, :], g_sem.at[h])

    barrier = pltpu.get_barrier_semaphore()
    for d in range(1, n_re):
        pl.semaphore_signal(barrier, inc=1, device_id={"re": lax.rem(x + d, n_re)}, device_id_type=MESH)

    @pl.when(z > 0)
    def _():
        pl.semaphore_signal(barrier, inc=1, device_id={"pb": z - 1}, device_id_type=MESH)

    @pl.when(z < n_pb - 1)
    def _():
        pl.semaphore_signal(barrier, inc=1, device_id={"pb": z + 1}, device_id_type=MESH)

    el_copy = pltpu.make_async_copy(el_hbm, el_ref, el_sem)
    el_copy.start()
    for h in range(halves):
        g_copy(h).start()

    rows, cols = k_all * GROUP, GROUP * e_loc
    spread_k = (iota((rows, k_all), 0) // GROUP == iota((rows, k_all), 1)).astype(BF16)
    spread_e = (iota((e_all, cols), 0) == x * e_loc + iota((e_all, cols), 1) % e_loc).astype(BF16)
    same_p = iota((rows, cols), 0) % GROUP == iota((rows, cols), 1) // e_loc

    def spread(table):
        t = jnp.dot(spread_k, table, preferred_element_type=F32).astype(BF16)
        t = jnp.dot(t, spread_e, preferred_element_type=F32)
        return jnp.where(same_p, t, 0.0)

    el_copy.wait()
    cos_e = spread(el_ref[0])
    sin_e = spread(el_ref[1])
    el_block[0:rows, 0:cols] = cos_e.astype(BF16)
    el_block[0:rows, cols:] = (-sin_e).astype(BF16)
    el_block[rows:, 0:cols] = sin_e.astype(BF16)
    el_block[rows:, cols:] = cos_e.astype(BF16)

    def x_first_copy(h, d):
        there = pl.ds(pl.multiple_of(h * p_half, p_half), p_half)
        to = lax.rem(x + d, n_re)
        return pltpu.make_async_remote_copy(
            src_ref=x_first.at[to, there, :],
            dst_ref=x_first_recv.at[d - 1, there, :],
            send_sem=x_send.at[d - 1, h],
            recv_sem=x_got.at[d - 1, h],
            device_id={"re": to},
            device_id_type=MESH,
        )

    def x_copy(c, d):
        k, h = c // halves, c % halves
        there = pl.ds(pl.multiple_of(h * p_half, p_half), p_half)
        to = lax.rem(x + d, n_re)
        return pltpu.make_async_remote_copy(
            src_ref=part.at[to * k_own + k, there, :],
            dst_ref=x_recv.at[d - 1, k, there, :],
            send_sem=x_send.at[d - 1, c],
            recv_sem=x_got.at[d - 1, c],
            device_id={"re": to},
            device_id_type=MESH,
        )

    def z_copy(c, source, way):
        k, h = c // halves, c % halves
        there = pl.ds(pl.multiple_of(source * p_loc + h * p_half, p_half), p_half)
        block = gath.at[k, there, :]
        return pltpu.make_async_remote_copy(
            src_ref=block,
            dst_ref=block,
            send_sem=z_send.at[way, c, source],
            recv_sem=z_got.at[c, source],
            device_id={"pb": z + 1 if way else z - 1},
            device_id_type=MESH,
        )

    def own_step(t):
        k, h = t // halves, t % halves
        there = pl.ds(pl.multiple_of(h * p_half, p_half), p_half)
        mine = pl.ds(pl.multiple_of(z * p_loc + h * p_half, p_half), p_half)

        @pl.when(t < halves)
        def _():
            total = part[x * k_own, there, :]
            for d in range(1, n_re):
                x_first_copy(t, d).wait_recv()
                total = total + x_first_recv[d - 1, there, :].astype(F32)
            gath[0, mine, :] = total.astype(BF16)

        @pl.when(t >= halves)
        def _():
            total = part[x * k_own + k, there, :]
            for d in range(1, n_re):
                x_copy(t, d).wait_recv()
                total = total + x_recv[d - 1, k, there, :]
            gath[k, mine, :] = total.astype(BF16)

        @pl.when(z > 0)
        def _():
            z_copy(t, z, 0).start()

        @pl.when(z < n_pb - 1)
        def _():
            z_copy(t, z, 1).start()

    for h in range(halves):
        g_copy(h).wait()

        @pl.loop(h * (p_half // GROUP // PAIR), (h + 1) * (p_half // GROUP // PAIR), unroll=UNROLL)
        def _(j):
            sides = []
            for side in range(PAIR):
                at = pl.ds(pl.multiple_of((j * PAIR + side) * cols, cols), cols)
                sides.append(jnp.concatenate([g[0, at, :], g[1, at, :]], axis=0))
            both = jnp.concatenate(sides, axis=1)
            res = jnp.dot(el_block[...], both, preferred_element_type=F32)
            for side in range(PAIR):
                p_at = pl.ds(pl.multiple_of((j * PAIR + side) * GROUP, GROUP), GROUP)
                for c in range(2):
                    for k in range(k_all):
                        first = (c * k_all + k) * GROUP
                        part[k, p_at, c * b:(c + 1) * b] = res[first:first + GROUP, side * b:(side + 1) * b]

        if h == 0:
            n_meet = n_re - 1 + jnp.where(z > 0, 1, 0) + jnp.where(z < n_pb - 1, 1, 0)
            pl.semaphore_wait(barrier, n_meet)
        there = pl.ds(h * p_half, p_half)
        for r in range(n_re):
            x_first[r, there, :] = part[r * k_own, there, :].astype(BF16)
        for d in range(1, n_re):
            x_first_copy(h, d).start()
        if h >= halves - AHEAD:
            own_step(h - (halves - AHEAD))
    for c in range(halves, chunks):
        for d in range(1, n_re):
            x_copy(c, d).start()
    ph_copy = pltpu.make_async_copy(ph_hbm, ph, ph_sem)
    ph_copy.start()

    @pl.loop(AHEAD, chunks + (n_pb - 2) * (1 + SLACK))
    def _(t):
        @pl.when(t < chunks)
        def _():
            own_step(t)

        for d in range(1, n_pb - 1):
            c = t - d * (1 + SLACK)
            ok = (c >= 0) & (c < chunks)

            @pl.when(ok & (z - d >= 0) & (z < n_pb - 1))
            def _():
                z_copy(c, z - d, 1).wait_recv()
                z_copy(c, z - d, 1).start()

            @pl.when(ok & (z + d < n_pb) & (z > 0))
            def _():
                z_copy(c, z + d, 0).wait_recv()
                z_copy(c, z + d, 0).start()

    ph_copy.wait()
    q_tile = min(256, q_loc)

    @pl.loop(0, k_own)
    def _(k):
        for h in range(halves):
            c = k * halves + h
            for s in range(n_pb):
                @pl.when(((s < z) & (z == n_pb - 1)) | ((s > z) & (z == 0)))
                def _():
                    z_copy(c, s, 0).wait_recv()

        @pl.loop(0, q_loc // q_tile)
        def _(i):
            at = pl.ds(pl.multiple_of(i * q_tile, q_tile), q_tile)
            data = gath[k]
            by_cos = jnp.dot(ph[0, at, :], data, preferred_element_type=F32)
            by_sin = jnp.dot(ph[1, at, :], data, preferred_element_type=F32)
            out[k, 0, at, :] = by_cos[:, :b] - by_sin[:, b:]
            out[k, 1, at, :] = by_cos[:, b:] + by_sin[:, :b]

    @pl.loop(0, chunks)
    def _(c):
        for d in range(1, n_re):
            @pl.when(c < halves)
            def _():
                x_first_copy(c, d).wait_send()

            @pl.when(c >= halves)
            def _():
                x_copy(c, d).wait_send()
        for s in range(n_pb):
            @pl.when((s >= z) & (z > 0))
            def _():
                z_copy(c, s, 0).wait_send()

            @pl.when((s <= z) & (z < n_pb - 1))
            def _():
                z_copy(c, s, 1).wait_send()


def body(n_re, n_pb, g_wann, phonon_phase, electron_phase):
    _, p_loc, e_loc, b = g_wann.shape
    _, q_loc, p_all = phonon_phase.shape
    k_all = electron_phase.shape[1]
    k_own = k_all // n_re
    halves = 2
    chunks = k_own * halves
    g = g_wann.reshape(2, p_loc * e_loc, b)
    far = pl.BlockSpec(memory_space=pltpu.HBM)
    near = pl.BlockSpec(memory_space=pltpu.VMEM)
    return pl.pallas_call(
        functools.partial(kernel, n_re, n_pb, halves),
        out_shape=jax.ShapeDtypeStruct((k_own, 2, q_loc, b), F32),
        in_specs=[far, far, far],
        out_specs=near,
        scratch_shapes=[
            pltpu.VMEM(g.shape, BF16),
            pltpu.VMEM(phonon_phase.shape, BF16),
            pltpu.VMEM(electron_phase.shape, BF16),
            pltpu.VMEM((2 * k_all * GROUP, 2 * GROUP * e_loc), BF16),
            pltpu.VMEM((k_all, p_loc, 2 * b), F32),
            pltpu.VMEM((n_re, p_loc, 2 * b), BF16),
            pltpu.VMEM((n_re - 1, p_loc, 2 * b), BF16),
            pltpu.VMEM((n_re - 1, k_own, p_loc, 2 * b), F32),
            pltpu.VMEM((k_own, p_all, 2 * b), BF16),
            pltpu.SemaphoreType.DMA((halves,)),
            pltpu.SemaphoreType.DMA,
            pltpu.SemaphoreType.DMA,
            pltpu.SemaphoreType.DMA((n_re - 1, chunks)),
            pltpu.SemaphoreType.DMA((n_re - 1, chunks)),
            pltpu.SemaphoreType.DMA((2, chunks, n_pb)),
            pltpu.SemaphoreType.DMA((chunks, n_pb)),
        ],
        compiler_params=pltpu.CompilerParams(
            collective_id=0, has_side_effects=True, vmem_limit_bytes=24 * 1024 * 1024
        ),
    )(*(pltpu.with_memory_space_constraint(a, pltpu.HBM) for a in (g, phonon_phase, electron_phase)))


def solution(mesh):
    placed = (P(None, "pb", ("grp", "re"), "ka"), P(None, "pb", None), P())
    return jax.shard_map(
        functools.partial(body, mesh.shape["re"], mesh.shape["pb"]),
        mesh=mesh,
        in_specs=placed,
        out_specs=P(("grp", "re"), None, "pb", "ka"),
        check_vma=False,
    )
```
